32 devices in a mesh: wide: 8 (over y, x, core), narrow: 4 (over z).
Axes of the slice: x: 2, y: 2, z: 4, core: 2. Of those that a mesh axis runs over, the one named last changes fastest.
Arguments:
- hamiltonian_tiles: float32 [12288, 6144], P('wide', 'narrow'), may hold values from -0.0546875 to 0.0546875
- row_columns: int32 [8, 4], P('wide'), may hold values from 0 to 7, as said below
- start_vectors: float32 [12288, 128], P(('wide', 'narrow')), may hold values from -60 to 60
Outputs:
- new_vectors: float32 [12288, 128], P(('wide', 'narrow'))
The draws below stay inside these ranges and needn't reach their ends.
Inputs may be any that keep to these rules, and one draw needn't show every extreme that they name: For block row r = w + j // 4, row_columns[w, j] = (r + d) mod 8, with d = 0 where j % 4 = 0 and, for the other tiles of that block row, distinct d between 1 and 7; a block's mirror may also be stored.
All inputs are finite; a program needn't handle non-finite values.
Results may differ from the reference program's by a relative error of at most 0.0003.
Values sent between devices are 32-bit elements; how exact they have to be, the bound alone decides.
A program may use at most 64 MiB of HBM per device.

```python
import jax
import jax.numpy as jnp
from jax import lax

B = 1536
K = 128
ITERS = 2
NS_STEPS = 5
TILES_ROW = 4
NB = 8
N_WIDE = 8
N_NARROW = 4


def draw_row_columns(key, part):
    rows_group = N_NARROW // TILES_ROW
    blocks = N_WIDE * rows_group
    half = blocks // 2
    count = blocks - 2
    candidates = jnp.arange(count, dtype=jnp.int32) + 1
    scores = jax.random.randint(jax.random.fold_in(key, 11), (blocks, count), 0, 1048576)
    scores = scores * blocks + jnp.arange(count, dtype=jnp.int32)[None, :]
    scores = jnp.where(candidates[None, :] == half, 2000000000, scores)
    order = jnp.argsort(scores, axis=1).astype(jnp.int32)
    randoms = order[:, :TILES_ROW - 3] + 1
    fixed = jnp.concatenate([jnp.zeros((blocks, 1), jnp.int32), jnp.full((blocks, 1), half, jnp.int32), jnp.full((blocks, 1), blocks - 1, jnp.int32)], axis=1)
    offsets = jnp.concatenate([fixed, randoms], axis=1)
    rows = jnp.arange(blocks, dtype=jnp.int32)[:, None]
    return ((rows + offsets) % blocks).reshape(N_WIDE, N_NARROW).astype(jnp.int32)


def draw_start_vectors(key, part):
    column_key = jax.random.fold_in(key, 21)
    entry_key = jax.random.fold_in(key, 22)
    column_scale = 10.0 ** jax.random.uniform(column_key, (1, K), jnp.float32, 0.0, 1.0)
    entries = jax.random.normal(entry_key, (NB * B, K), jnp.float32)
    values = entries * column_scale
    return jnp.clip(values, -60.0, 60.0).astype(jnp.float32)


def level_of(own_key, shape, cuts, least, largest):
    def one(position, blocks):
        draws = jax.random.uniform(jax.random.fold_in(jax.random.fold_in(own_key, 6), position), (blocks,), jnp.float32, least / len(cuts), largest / len(cuts))
        return jnp.repeat(jnp.exp(draws), shape[position] // blocks).reshape((-1,) + (1,) * (len(shape) - position - 1))

    loudness = one(*cuts[0])
    for cut in cuts[1:]:
        loudness = loudness * one(*cut)
    return loudness


def bell_draw(rng, dims, deviation, bound, cuts=(), kind=jnp.bfloat16):
    drawn = jax.random.normal(rng, dims, jnp.float32) * deviation
    if len(cuts) > 0:
        drawn = level_of(rng, dims, cuts, -0.22, 0.18) * drawn
    return jnp.clip(drawn, min=-bound, max=bound).astype(kind)


def setup_inputs(seed: int = 0) -> dict:
    seeds = jax.random.split(jax.random.key(seed), 4)
    return {
        "hamiltonian_tiles": bell_draw(seeds[0], (N_WIDE * B, N_NARROW * B), (2 * B * TILES_ROW) ** -0.5, 0.0546875, ((0, 8), (1, 4)), jnp.float32),
        "row_columns": draw_row_columns(jax.random.fold_in(seeds[3], 71), 0),
        "start_vectors": draw_start_vectors(jax.random.fold_in(seeds[3], 71), 0),
    }


def apply_hamiltonian(tiles, columns, vectors):
    rows_group = N_NARROW // TILES_ROW
    blocks = vectors.reshape(NB, B, K)
    grouped = tiles.reshape(N_WIDE, B, N_NARROW, B)
    owned = blocks.reshape(N_WIDE, rows_group, B, K)

    def one_group(carry, inputs):
        group_tiles, group_cols, own_blocks = inputs
        quad = group_tiles.reshape(B, rows_group, TILES_ROW, B)
        cols = group_cols.astype(jnp.int32).reshape(rows_group, TILES_ROW)
        column_blocks = blocks[cols]
        direct = jnp.einsum('iqtj,qtjk->qik', quad, column_blocks, precision=lax.Precision.HIGHEST)
        transposed = jnp.einsum('iqtj,qik->qtjk', quad, own_blocks, precision=lax.Precision.HIGHEST)
        carry = carry.at[cols.reshape(N_NARROW)].add(transposed.reshape(N_NARROW, B, K))
        return (carry, direct)
    zeros = jnp.zeros((NB, B, K), jnp.float32)
    moved, direct_rows = lax.scan(one_group, zeros, (grouped, columns, owned))
    return (direct_rows.reshape(NB, B, K) + moved).reshape(NB * B, K)

def orthonormalize(product, gram):
    identity = jnp.eye(K, dtype=jnp.float32)
    scale = jnp.sqrt(jnp.sum(gram * gram) + 1e-06)
    current = gram / scale
    inverse = identity
    for repeat in range(NS_STEPS):
        middle = 1.5 * identity - 0.5 * jnp.dot(inverse, current, precision=lax.Precision.HIGHEST)
        current = jnp.dot(current, middle, precision=lax.Precision.HIGHEST)
        inverse = jnp.dot(middle, inverse, precision=lax.Precision.HIGHEST)
    return jnp.dot(product, inverse, precision=lax.Precision.HIGHEST) * jnp.sqrt(NB * B / scale)

def reference(hamiltonian_tiles, row_columns, start_vectors):
    vectors = start_vectors
    for repeat in range(ITERS):
        product = apply_hamiltonian(hamiltonian_tiles, row_columns, vectors)
        gram = jnp.dot(product.T, product, precision=lax.Precision.HIGHEST)
        vectors = orthonormalize(product, gram)
    return vectors
```

```python
import functools

import jax
import jax.numpy as jnp
from jax import lax
from jax.experimental import pallas as pl
from jax.experimental.pallas import tpu as pltpu
from jax.sharding import PartitionSpec as P

ITERS = 2
NS_STEPS = 5
HIGHEST = lax.Precision.HIGHEST


def flip(x, mask):
    bit = 1
    while bit <= mask:
        if mask & bit:
            x = x + bit * (1 - 2 * ((x // bit) % 2))
        bit *= 2
    return x


def bits_of(count):
    bits = count.bit_length() - 1
    assert count == 1 << bits
    return bits


def orders(wide):
    bits = list(range(1, bits_of(wide)))
    return bits + [0], bits[::-1] + [0]


def position(relative, order):
    return sum(((relative >> bit) & 1) << place for place, bit in enumerate(order))


def inverse_root(gram, total):
    size = gram.shape[0]
    row = lax.broadcasted_iota(jnp.int32, (size, size), 0)
    column = lax.broadcasted_iota(jnp.int32, (size, size), 1)
    identity = jnp.where(row == column, 1.0, 0.0).astype(jnp.float32)
    square = jnp.sum(gram * gram, axis=1, keepdims=True)
    scale = jnp.sqrt(jnp.sum(square, axis=0, keepdims=True) + 1e-06)
    current = gram / scale
    inverse = identity
    for repeat in range(NS_STEPS):
        if repeat == 0:
            middle = 1.5 * identity - 0.5 * current
        else:
            middle = 1.5 * identity - 0.5 * jnp.dot(inverse, current, precision=HIGHEST)
        if repeat < NS_STEPS - 1:
            current = jnp.dot(current, middle, precision=HIGHEST)
        inverse = middle if repeat == 0 else jnp.dot(middle, inverse, precision=HIGHEST)
    return inverse * jnp.sqrt(total / scale)


def split(x):
    high = x.astype(jnp.bfloat16)
    low = (x - high.astype(jnp.float32)).astype(jnp.bfloat16)
    return high, low


def kernel(wide, narrow, places, tile_hbm, start, out, stage, tile_hi, tile_lo, block,
           left, right, trans, direct, own, high, rowp, gath, pick, picked, tpart, dpart,
           placed, came, merged, last, grams, stage_sem, send_sem, recv_sem):
    me_w = lax.axis_index("wide")
    me_z = lax.axis_index("narrow")
    order = trans.shape[0]
    rows, width = own.shape[1], own.shape[2]
    half = rows // 2
    halves = narrow // 2
    wbits = bits_of(wide)
    hbits = bits_of(halves)
    two_orders = orders(wide)
    mate = flip(me_z, 1)
    wide_peers = [{"wide": flip(me_w, 1 << bit), "narrow": me_z} for bit in range(wbits)]
    near_peers = [
        {"wide": me_w, "narrow": flip(me_z, 1 << bit)} for bit in range(bits_of(narrow))
    ]

    barrier = pltpu.get_barrier_semaphore()
    for peer in wide_peers + near_peers:
        pl.semaphore_signal(
            barrier, inc=1, device_id=peer, device_id_type=pl.DeviceIdType.MESH
        )

    stage_rows = stage.shape[1]
    chunks = order // stage_rows

    def fetch(chunk):
        return pltpu.make_async_copy(
            tile_hbm.at[pl.ds(chunk * stage_rows, stage_rows)],
            stage.at[chunk % 2],
            stage_sem.at[chunk % 2],
        )

    fetch(0).start()
    if chunks > 1:
        fetch(1).start()
    pl.semaphore_wait(barrier, len(wide_peers) + len(near_peers))

    sent = []

    def send(source, target, peer):
        index = len(sent)
        copy = pltpu.make_async_remote_copy(
            src_ref=source,
            dst_ref=target,
            send_sem=send_sem.at[index],
            recv_sem=recv_sem.at[index],
            device_id=peer,
            device_id_type=pl.DeviceIdType.MESH,
        )
        copy.start()
        sent.append([copy, False])
        return len(sent) - 1

    def received(index):
        sent[index][0].wait_recv()

    def gone(index):
        if not sent[index][1]:
            sent[index][0].wait_send()
            sent[index][1] = True

    def natural(q):
        return pl.multiple_of(flip(me_z, q) * rows, rows)

    def load_tile():
        for chunk in range(chunks):
            fetch(chunk).wait()
            hi, lo = split(stage[chunk % 2])
            tile_hi[pl.ds(chunk * stage_rows, stage_rows), :] = hi
            tile_lo[pl.ds(chunk * stage_rows, stage_rows), :] = lo
            if chunk + 2 < chunks:
                fetch(chunk + 2).start()

    gram_peers = wide_peers + near_peers
    gram_state = {}

    def gram_begin(which, value):
        grams[which, 0] = value
        gram_state[which] = (0, send(grams.at[which, 0], grams.at[which, 1], gram_peers[0]))

    def gram_step(which):
        step, index = gram_state[which]
        received(index)
        total = grams[which, 2 * step] + grams[which, 2 * step + 1]
        step += 1
        if step == len(gram_peers):
            gram_state[which] = (step, None)
            return total
        grams[which, 2 * step] = total
        gram_state[which] = (
            step, send(grams.at[which, 2 * step], grams.at[which, 2 * step + 1], gram_peers[step])
        )
        return None

    total_rows = float(wide * order)
    step_of_columns = 256
    placed_sends = []
    merged_sends = []
    first_root = None

    for it in range(ITERS):
        high[it, 0] = start[...] if it == 0 else own[it]
        source = start if it == 0 else high.at[it, 0]
        far = []
        if halves > 1:
            far.append(send(source, high.at[it, 1], near_peers[1]))
        row_in = [None] * halves
        gathers = {}

        def begin(r):
            base = start if (it == 0 and r == 0) else high.at[it, r]
            row_in[r] = send(base, rowp.at[it, r], near_peers[0])
            for side in range(2):
                gath[it, side, r, 0] = high[it, r, pl.ds(side * half, half), :]
                gathers[r, side, 0] = send(
                    base.at[pl.ds(side * half, half)],
                    gath.at[it, side, r, 1],
                    wide_peers[two_orders[side][0]],
                )

        def advance(r, step):
            for side in range(2):
                received(gathers[r, side, step - 1])
                if step < wbits:
                    count = 1 << step
                    gathers[r, side, step] = send(
                        gath.at[it, side, r, pl.ds(0, count)],
                        gath.at[it, side, r, pl.ds(count, count)],
                        wide_peers[two_orders[side][step]],
                    )

        pick_in = [None] * halves

        def chosen(r, side, column):
            value = gath[it, side, r, 0]
            for p in range(1, wide):
                value = jnp.where(places[side, column] == p, gath[it, side, r, p], value)
            return value

        def choose(r):
            for side in range(2):
                pick[it, r, pl.ds(side * half, half), :] = chosen(r, side, mate)
            pick_in[r] = send(pick.at[it, r], picked.at[it, r], near_peers[0])

        def ready(r):
            if r == 0:
                return
            step = r.bit_length() - 1
            if r == 1 << step:
                received(far[step])
                if step + 1 < hbits:
                    count = 1 << (step + 1)
                    far.append(send(
                        high.at[it, pl.ds(0, count)],
                        high.at[it, pl.ds(count, count)],
                        near_peers[step + 2],
                    ))

        def transposed_terms():
            for r in range(halves):
                received(row_in[r])
                block[pl.ds(natural(2 * r), rows), :] = high[it, r]
                block[pl.ds(natural(2 * r + 1), rows), :] = rowp[it, r]
            turned = block[...].T
            hi, lo = split(turned)
            left[pl.ds(0, width), :] = hi
            left[pl.ds(width, width), :] = lo

            def body(chunk, carry):
                at = pl.multiple_of(chunk * step_of_columns, step_of_columns)
                both = jnp.dot(
                    left[...], tile_hi[:, pl.ds(at, step_of_columns)],
                    preferred_element_type=jnp.float32,
                )
                rest = jnp.dot(
                    left[pl.ds(0, width), :], tile_lo[:, pl.ds(at, step_of_columns)],
                    preferred_element_type=jnp.float32,
                )
                trans[pl.ds(at, step_of_columns), :] = (both[:width] + (both[width:] + rest)).T
                return carry

            lax.fori_loop(0, order // step_of_columns, body, 0)

        t_out = []
        d_out = []

        def direct_terms():
            for r in range(halves):
                received(pick_in[r])
                for side in range(2):
                    block[pl.ds(natural(2 * r) + side * half, half), :] = chosen(r, side, me_z)
                block[pl.ds(natural(2 * r + 1), rows), :] = picked[it, r]
            hi, lo = split(block[...])
            right[:, pl.ds(0, width)] = hi
            right[:, pl.ds(width, width)] = lo

            def body(chunk, carry):
                at = pl.multiple_of(chunk * step_of_columns, step_of_columns)
                both = jnp.dot(
                    tile_hi[pl.ds(at, step_of_columns), :], right[...],
                    preferred_element_type=jnp.float32,
                )
                rest = jnp.dot(
                    tile_lo[pl.ds(at, step_of_columns), :], right[:, pl.ds(0, width)],
                    preferred_element_type=jnp.float32,
                )
                direct[pl.ds(at, step_of_columns), :] = both[:, :width] + (both[:, width:] + rest)
                return carry

            lax.fori_loop(0, order // step_of_columns, body, 0)

        for time in range(halves + wbits + 1):
            for r in range(halves):
                step = time - r
                if step == 0:
                    ready(r)
                    begin(r)
                elif 0 < step <= wbits:
                    advance(r, step)
                    if step == wbits:
                        choose(r)
            if it == 0 and time == 0:
                load_tile()
            if it > 0 and 0 < time:
                if gram_state[0][1] is not None:
                    total = gram_step(0)
            if time == max(wbits, halves - 1):
                for index in t_out:
                    gone(index)
                transposed_terms()
                for r in range(halves - 1, -1, -1):
                    t_out.append(send(
                        trans.at[pl.ds(natural(2 * r + 1), rows)], tpart.at[it, r], near_peers[0]
                    ))
        direct_terms()
        for r in range(halves - 1, -1, -1):
            d_out.append(send(
                direct.at[pl.ds(natural(2 * r + 1), rows)], dpart.at[it, r], near_peers[0]
            ))
        if it > 0:
            while gram_state[0][1] is not None:
                total = gram_step(0)

        for index in placed_sends:
            gone(index)
        placed_sends = []
        sums = {}

        def put(r, side, first, count):
            mine = trans[pl.ds(natural(2 * r) + side * half, half), :]
            other = tpart[it, r, pl.ds(side * half, half), :]
            for p in range(first, first + count):
                placed[side, r, p] = jnp.where(places[side, me_z] == p, mine, 0.0) + jnp.where(
                    places[side, mate] == p, other, 0.0
                )

        def pass_on(r, side, step):
            count = 1 << step
            index = send(
                placed.at[side, r, pl.ds(count, count)],
                came.at[it, side, r, pl.ds(count, count)],
                wide_peers[two_orders[side][step]],
            )
            sums[r, side, step] = index
            placed_sends.append(index)

        for time in range(halves + wbits + 1):
            for turn in range(halves):
                r = halves - 1 - turn
                step = wbits - 1 - (time - turn)
                if step == wbits - 1:
                    received(t_out[turn])
                    for side in range(2):
                        put(r, side, wide // 2, wide // 2)
                        pass_on(r, side, step)
                    for side in range(2):
                        put(r, side, 0, wide // 2)
                elif -1 <= step < wbits - 1:
                    count = 1 << (step + 1)
                    for side in range(2):
                        received(sums[r, side, step + 1])
                        for p in range(count - 1, -1, -1):
                            placed[side, r, p] = placed[side, r, p] + came[it, side, r, count + p]
                        if step >= 0:
                            pass_on(r, side, step)
            if it > 0 and time == 0:
                first_root = inverse_root(total, total_rows)
                grams[0, 0 + 2 * len(gram_peers)] = first_root

        for turn in range(halves):
            r = halves - 1 - turn
            received(d_out[turn])
            for side in range(2):
                part = pl.ds(side * half, half)
                merged[it, r, part, :] = (
                    placed[side, r, 0]
                    + direct[pl.ds(natural(2 * r) + side * half, half), :]
                    + dpart[it, r, part, :]
                )
        for bit in range(hbits - 1, -1, -1):
            count = 1 << bit
            index = send(
                merged.at[it, pl.ds(count, count)],
                last.at[it, pl.ds(count, count)],
                near_peers[bit + 1],
            )
            received(index)
            for r in range(count):
                merged[it, r] = merged[it, r] + last[it, count + r]
        for index in t_out + d_out:
            gone(index)
        product = merged[it, 0]
        own[it + 1] = product
        turned = product.T
        gram_begin(it, jnp.dot(turned, product, precision=HIGHEST))

    root = grams[0, 2 * len(gram_peers)]
    total = None
    while total is None:
        total = gram_step(1)
    gram = jnp.dot(root.T, jnp.dot(total, root, precision=HIGHEST), precision=HIGHEST)
    root = jnp.dot(root, inverse_root(gram, total_rows), precision=HIGHEST)
    out[...] = jnp.dot(own[ITERS], root, precision=HIGHEST)
    for index in range(len(sent)):
        gone(index)


def on_device(hamiltonian_tiles, row_columns, start_vectors):
    wide, narrow = lax.axis_size("wide"), lax.axis_size("narrow")
    order = hamiltonian_tiles.shape[0]
    rows, width = start_vectors.shape
    assert rows * narrow == order
    halves = narrow // 2
    wbits, nbits = bits_of(wide), bits_of(narrow)
    relative = jnp.bitwise_xor(row_columns[0], lax.axis_index("wide").astype(jnp.int32))
    places = jnp.stack([position(relative, order_) for order_ in orders(wide)])
    copies = ITERS * (
        2 * (nbits - 1) + 4 * halves * wbits + 4 * halves
    ) + ITERS * (wbits + nbits)
    f32, bf16 = jnp.float32, jnp.bfloat16
    stage_rows = order // 6
    return pl.pallas_call(
        functools.partial(kernel, wide, narrow),
        out_shape=jax.ShapeDtypeStruct((rows, width), f32),
        in_specs=[
            pl.BlockSpec(memory_space=pltpu.SMEM),
            pl.BlockSpec(memory_space=pl.ANY),
            pl.BlockSpec(memory_space=pltpu.VMEM),
        ],
        out_specs=pl.BlockSpec(memory_space=pltpu.VMEM),
        scratch_shapes=[
            pltpu.VMEM((2, stage_rows, order), f32),
            pltpu.VMEM((order, order), bf16),
            pltpu.VMEM((order, order), bf16),
            pltpu.VMEM((order, width), f32),
            pltpu.VMEM((2 * width, order), bf16),
            pltpu.VMEM((order, 2 * width), bf16),
            pltpu.VMEM((order, width), f32),
            pltpu.VMEM((order, width), f32),
            pltpu.VMEM((ITERS + 1, rows, width), f32),
            pltpu.VMEM((ITERS, halves, rows, width), f32),
            pltpu.VMEM((ITERS, halves, rows, width), f32),
            pltpu.VMEM((ITERS, 2, halves, wide, rows // 2, width), f32),
            pltpu.VMEM((ITERS, halves, rows, width), f32),
            pltpu.VMEM((ITERS, halves, rows, width), f32),
            pltpu.VMEM((ITERS, halves, rows, width), f32),
            pltpu.VMEM((ITERS, halves, rows, width), f32),
            pltpu.VMEM((2, halves, wide, rows // 2, width), f32),
            pltpu.VMEM((ITERS, 2, halves, wide, rows // 2, width), f32),
            pltpu.VMEM((ITERS, halves, rows, width), f32),
            pltpu.VMEM((ITERS, halves, rows, width), f32),
            pltpu.VMEM((ITERS, 2 * (wbits + nbits) + 1, width, width), f32),
            pltpu.SemaphoreType.DMA((2,)),
            pltpu.SemaphoreType.DMA((copies,)),
            pltpu.SemaphoreType.DMA((copies,)),
        ],
        compiler_params=pltpu.CompilerParams(
            collective_id=0, has_side_effects=True, vmem_limit_bytes=67043328
        ),
    )(places, hamiltonian_tiles, start_vectors)


def solution(mesh):
    return jax.shard_map(
        on_device,
        mesh=mesh,
        in_specs=(P("wide", "narrow"), P("wide", None), P(("wide", "narrow"), None)),
        out_specs=P(("wide", "narrow"), None),
        check_vma=False,
    )
```

```python
import functools

import jax
import jax.numpy as jnp
from jax import lax
from jax.experimental import pallas as pl
from jax.experimental.pallas import tpu as pltpu
from jax.sharding import PartitionSpec as P

ITERS = 2
NS_STEPS = 5
HIGHEST = lax.Precision.HIGHEST


def flip(x, mask):
    bit = 1
    while bit <= mask:
        if mask & bit:
            x = x + bit * (1 - 2 * ((x // bit) % 2))
        bit *= 2
    return x


def bits_of(count):
    bits = count.bit_length() - 1
    assert count == 1 << bits
    return bits


def orders(wide):
    bits = list(range(1, bits_of(wide)))
    return bits + [0], bits[::-1] + [0]


def position(relative, order):
    return sum(((relative >> bit) & 1) << place for place, bit in enumerate(order))


def inverse_root(gram, total):
    size = gram.shape[0]
    row = lax.broadcasted_iota(jnp.int32, (size, size), 0)
    column = lax.broadcasted_iota(jnp.int32, (size, size), 1)
    identity = jnp.where(row == column, 1.0, 0.0).astype(jnp.float32)
    square = jnp.sum(gram * gram, axis=1, keepdims=True)
    scale = jnp.sqrt(jnp.sum(square, axis=0, keepdims=True) + 1e-06)
    current = gram / scale
    inverse = identity
    for repeat in range(NS_STEPS):
        if repeat == 0:
            middle = 1.5 * identity - 0.5 * current
        else:
            middle = 1.5 * identity - 0.5 * jnp.dot(inverse, current, precision=HIGHEST)
        if repeat < NS_STEPS - 1:
            current = jnp.dot(current, middle, precision=HIGHEST)
        inverse = middle if repeat == 0 else jnp.dot(middle, inverse, precision=HIGHEST)
    return inverse * jnp.sqrt(total / scale)


def split(x):
    high = x.astype(jnp.bfloat16)
    low = (x - high.astype(jnp.float32)).astype(jnp.bfloat16)
    return high, low


def kernel(wide, narrow, out_cuts, places, tile_hbm, start, out, stage, tile_hi, tile_lo, block, columns,
           left, right, trans, direct, own, high, rowp, gath, pick, picked, tpart, dpart,
           placed, came, merged, last, grams, stage_sem, send_sem, recv_sem):
    me_w = lax.axis_index("wide")
    me_z = lax.axis_index("narrow")
    order = trans.shape[0]
    rows, width = own.shape[1], own.shape[2]
    halves = narrow // 2
    wbits = bits_of(wide)
    hbits = bits_of(halves)
    two_orders = orders(wide)
    mate = flip(me_z, 1)
    wide_peers = [{"wide": flip(me_w, 1 << bit), "narrow": me_z} for bit in range(wbits)]
    near_peers = [
        {"wide": me_w, "narrow": flip(me_z, 1 << bit)} for bit in range(bits_of(narrow))
    ]

    barrier = pltpu.get_barrier_semaphore()
    for peer in wide_peers + near_peers:
        pl.semaphore_signal(
            barrier, inc=1, device_id=peer, device_id_type=pl.DeviceIdType.MESH
        )

    stage_rows = stage.shape[1]
    chunks = order // stage_rows

    def fetch(chunk):
        return pltpu.make_async_copy(
            tile_hbm.at[pl.ds(chunk * stage_rows, stage_rows)],
            stage.at[chunk % 2],
            stage_sem.at[chunk % 2],
        )

    fetch(0).start()
    if chunks > 1:
        fetch(1).start()
    pl.semaphore_wait(barrier, len(wide_peers) + len(near_peers))

    sent = []

    def send(source, target, peer):
        index = len(sent)
        copy = pltpu.make_async_remote_copy(
            src_ref=source,
            dst_ref=target,
            send_sem=send_sem.at[index],
            recv_sem=recv_sem.at[index],
            device_id=peer,
            device_id_type=pl.DeviceIdType.MESH,
        )
        copy.start()
        sent.append([copy, False])
        return len(sent) - 1

    def received(index):
        sent[index][0].wait_recv()

    def gone(index):
        if not sent[index][1]:
            sent[index][0].wait_send()
            sent[index][1] = True

    def natural(q):
        return pl.multiple_of(flip(me_z, q) * rows, rows)

    def load_chunk(chunk):
        fetch(chunk).wait()
        hi, lo = split(stage[chunk % 2])
        tile_hi[pl.ds(chunk * stage_rows, stage_rows), :] = hi
        tile_lo[pl.ds(chunk * stage_rows, stage_rows), :] = lo
        if chunk + 2 < chunks:
            fetch(chunk + 2).start()

    gram_peers = wide_peers + near_peers
    gram_state = {}

    def gram_begin(which, value):
        grams[which, 0] = value
        gram_state[which] = (0, send(grams.at[which, 0], grams.at[which, 1], gram_peers[0]))

    def gram_step(which):
        step, index = gram_state[which]
        received(index)
        total = grams[which, 2 * step] + grams[which, 2 * step + 1]
        step += 1
        if step == len(gram_peers):
            gram_state[which] = (step, None)
            return total
        grams[which, 2 * step] = total
        gram_state[which] = (
            step, send(grams.at[which, 2 * step], grams.at[which, 2 * step + 1], gram_peers[step])
        )
        return None

    total_rows = float(wide * order)
    step_of_columns = 256
    cuts = out_cuts
    piece = rows // cuts
    part = piece // 2
    units = [(r, c) for r in range(halves) for c in range(cuts)]
    back_units = [(r, c) for r in range(halves - 1, -1, -1) for c in range(cuts)]
    placed_sends = []
    total = None
    loaded = 0

    def whole_piece(c):
        return pl.ds(c * piece, piece)

    def side_rows(side):
        return pl.ds(side * part, part)

    for it in range(ITERS):
        far = {}
        row_in = {}
        pick_in = {}
        gathers = {}
        t_out = {}
        d_out = {}
        sums = {}
        ends = {}

        high[it, 0] = start[...] if it == 0 else own[it]
        source = start if it == 0 else high.at[it, 0]
        if halves > 1:
            for c in range(cuts):
                far[0, c] = send(
                    source.at[whole_piece(c)], high.at[it, 1, whole_piece(c)], near_peers[1]
                )

        def ready(r, c):
            if r == 0:
                return
            step = r.bit_length() - 1
            if r == 1 << step:
                received(far[step, c])
                if step + 1 < hbits:
                    count = 1 << (step + 1)
                    far[step + 1, c] = send(
                        high.at[it, pl.ds(0, count), whole_piece(c)],
                        high.at[it, pl.ds(count, count), whole_piece(c)],
                        near_peers[step + 2],
                    )

        def begin(r, c):
            base = source if r == 0 else high.at[it, r]
            for side in (2 * c, 2 * c + 1):
                gathers[r, side, 0] = send(
                    base.at[side_rows(side)],
                    gath.at[it, side, r, 1],
                    wide_peers[two_orders[side % 2][0]],
                )
            row_in[r, c] = send(
                base.at[whole_piece(c)], rowp.at[it, r, whole_piece(c)], near_peers[0]
            )
            for side in (2 * c, 2 * c + 1):
                gath[it, side, r, 0] = high[it, r, side_rows(side), :]

        def advance(r, c, step):
            for side in (2 * c, 2 * c + 1):
                received(gathers[r, side, step - 1])
                if step < wbits:
                    count = 1 << step
                    gathers[r, side, step] = send(
                        gath.at[it, side, r, pl.ds(0, count)],
                        gath.at[it, side, r, pl.ds(count, count)],
                        wide_peers[two_orders[side % 2][step]],
                    )

        def chosen(r, side, column):
            value = gath[it, side, r, 0]
            for p in range(1, wide):
                value = jnp.where(places[side % 2, column] == p, gath[it, side, r, p], value)
            return value

        def choose(r, c):
            for side in (2 * c, 2 * c + 1):
                pick[it, r, side_rows(side), :] = chosen(r, side, mate)
            pick_in[r, c] = send(
                pick.at[it, r, whole_piece(c)], picked.at[it, r, whole_piece(c)], near_peers[0]
            )
            for side in (2 * c, 2 * c + 1):
                columns[pl.ds(natural(2 * r) + side * part, part), :] = chosen(r, side, me_z)

        def transposed_terms():
            for r, c in units:
                received(row_in[r, c])
            for r in range(halves):
                block[pl.ds(natural(2 * r), rows), :] = high[it, r]
                block[pl.ds(natural(2 * r + 1), rows), :] = rowp[it, r]
            hi, lo = split(block[...].T)
            left[pl.ds(0, width), :] = hi
            left[pl.ds(width, width), :] = lo

            def body(chunk, carry):
                at = pl.multiple_of(chunk * step_of_columns, step_of_columns)
                both = jnp.dot(
                    left[...], tile_hi[:, pl.ds(at, step_of_columns)],
                    preferred_element_type=jnp.float32,
                )
                rest = jnp.dot(
                    left[pl.ds(0, width), :], tile_lo[:, pl.ds(at, step_of_columns)],
                    preferred_element_type=jnp.float32,
                )
                trans[pl.ds(at, step_of_columns), :] = (both[:width] + (both[width:] + rest)).T
                return carry

            lax.fori_loop(0, order // step_of_columns, body, 0)

        def direct_rows(q):
            at = natural(q)
            both = jnp.dot(
                tile_hi[pl.ds(at, rows), :], right[...], preferred_element_type=jnp.float32
            )
            rest = jnp.dot(
                tile_lo[pl.ds(at, rows), :], right[:, pl.ds(0, width)],
                preferred_element_type=jnp.float32,
            )
            direct[pl.ds(at, rows), :] = both[:, :width] + (both[:, width:] + rest)

        def send_rows(results, landing, group, r):
            for c in range(cuts):
                group[r, c] = send(
                    results.at[pl.ds(natural(2 * r + 1) + c * piece, piece)],
                    landing.at[it, r, whole_piece(c)],
                    near_peers[0],
                )

        def step_gram():
            return gram_step(it - 1) if it > 0 and gram_state[it - 1][1] is not None else None

        for time in range(len(units) + wbits):
            for place in range(len(units)):
                r, c = units[place]
                step = time - place
                if step == 0:
                    ready(r, c)
                    begin(r, c)
                elif 0 < step <= wbits:
                    advance(r, c, step)
                    if step == wbits:
                        choose(r, c)
            if it == 0 and loaded < chunks:
                load_chunk(loaded)
                loaded += 1
            if time % 2 == 1:
                found = step_gram()
                total = found if found is not None else total
        while loaded < chunks:
            load_chunk(loaded)
            loaded += 1

        transposed_terms()
        send_rows(trans, tpart, t_out, halves - 1)
        for r, c in units:
            received(pick_in[r, c])
        for r in range(halves):
            columns[pl.ds(natural(2 * r + 1), rows), :] = picked[it, r]
        hi, lo = split(columns[...])
        right[:, pl.ds(0, width)] = hi
        right[:, pl.ds(width, width)] = lo
        for r in range(halves - 1, -1, -1):
            direct_rows(2 * r + 1)
            send_rows(direct, dpart, d_out, r)
            if r > 0:
                send_rows(trans, tpart, t_out, r - 1)
        for r in range(halves - 1, -1, -1):
            direct_rows(2 * r)

        for index in placed_sends:
            gone(index)
        placed_sends = []

        def put(r, side, first, count):
            mine = trans[pl.ds(natural(2 * r) + side * part, part), :]
            other = tpart[it, r, side_rows(side), :]
            for p in range(first, first + count):
                placed[side, r, p] = jnp.where(
                    places[side % 2, me_z] == p, mine, 0.0
                ) + jnp.where(places[side % 2, mate] == p, other, 0.0)

        def pass_on(r, side, step):
            count = 1 << step
            index = send(
                placed.at[side, r, pl.ds(count, count)],
                came.at[it, side, r, pl.ds(count, count)],
                wide_peers[two_orders[side % 2][step]],
            )
            sums[r, side, step] = index
            placed_sends.append(index)

        def merge(r, c):
            received(d_out[r, c])
            for side in (2 * c, 2 * c + 1):
                at = side_rows(side)
                merged[it, r, at, :] = (
                    placed[side, r, 0]
                    + direct[pl.ds(natural(2 * r) + side * part, part), :]
                    + dpart[it, r, at, :]
                )
            if r >= max(1, halves // 2):
                ends[r, c] = send(
                    merged.at[it, r, whole_piece(c)],
                    last.at[it, r, whole_piece(c)],
                    near_peers[hbits],
                )

        for time in range(len(back_units) + wbits):
            for place in range(len(back_units)):
                r, c = back_units[place]
                step = wbits - 1 - (time - place)
                sides = (2 * c, 2 * c + 1)
                if step == wbits - 1:
                    received(t_out[r, c])
                    for side in sides:
                        put(r, side, wide // 2, wide // 2)
                        pass_on(r, side, step)
                    for side in sides:
                        put(r, side, 0, wide // 2)
                elif -1 <= step < wbits - 1:
                    count = 1 << (step + 1)
                    for side in sides:
                        received(sums[r, side, step + 1])
                        for p in range(count - 1, -1, -1):
                            placed[side, r, p] = placed[side, r, p] + came[it, side, r, count + p]
                        if step >= 0:
                            pass_on(r, side, step)
                    if step < 0:
                        merge(r, c)
            if time % 2 == 1:
                found = step_gram()
                total = found if found is not None else total
        if it > 0:
            while gram_state[it - 1][1] is not None:
                total = gram_step(it - 1)
            grams[0, 2 * len(gram_peers)] = inverse_root(total, total_rows)

        for r, c in ends:
            received(ends[r, c])
            merged[it, r - halves // 2, whole_piece(c), :] = (
                merged[it, r - halves // 2, whole_piece(c), :] + last[it, r, whole_piece(c), :]
            )
        for bit in range(hbits - 2, -1, -1):
            count = 1 << bit
            received(send(
                merged.at[it, pl.ds(count, count)],
                last.at[it, pl.ds(count, count)],
                near_peers[bit + 1],
            ))
            for r in range(count):
                merged[it, r] = merged[it, r] + last[it, count + r]
        for index in list(t_out.values()) + list(d_out.values()):
            gone(index)
        product = merged[it, 0]
        own[it + 1] = product
        gram_now = jnp.dot(product.T, product, precision=HIGHEST)
        gram_begin(it, gram_now)

    root = grams[0, 2 * len(gram_peers)]
    total = None
    while total is None:
        total = gram_step(1)
    gram = jnp.dot(root.T, jnp.dot(total, root, precision=HIGHEST), precision=HIGHEST)
    root = jnp.dot(root, inverse_root(gram, total_rows), precision=HIGHEST)
    out[...] = jnp.dot(own[ITERS], root, precision=HIGHEST)
    for index in range(len(sent)):
        gone(index)


def on_device(hamiltonian_tiles, row_columns, start_vectors):
    wide, narrow = lax.axis_size("wide"), lax.axis_size("narrow")
    order = hamiltonian_tiles.shape[0]
    rows, width = start_vectors.shape
    assert rows * narrow == order
    halves = narrow // 2
    wbits, nbits = bits_of(wide), bits_of(narrow)
    relative = jnp.bitwise_xor(row_columns[0], lax.axis_index("wide").astype(jnp.int32))
    places = jnp.stack([position(relative, order_) for order_ in orders(wide)])
    cuts = 2 if halves <= 2 else 1
    copies = ITERS * (
        2 * cuts * nbits + (4 * wbits + 5) * halves * cuts
    ) + ITERS * (wbits + nbits)
    f32, bf16 = jnp.float32, jnp.bfloat16
    stage_rows = order // 6
    return pl.pallas_call(
        functools.partial(kernel, wide, narrow, cuts),
        out_shape=jax.ShapeDtypeStruct((rows, width), f32),
        in_specs=[
            pl.BlockSpec(memory_space=pltpu.SMEM),
            pl.BlockSpec(memory_space=pl.ANY),
            pl.BlockSpec(memory_space=pltpu.VMEM),
        ],
        out_specs=pl.BlockSpec(memory_space=pltpu.VMEM),
        scratch_shapes=[
            pltpu.VMEM((2, stage_rows, order), f32),
            pltpu.VMEM((order, order), bf16),
            pltpu.VMEM((order, order), bf16),
            pltpu.VMEM((order, width), f32),
            pltpu.VMEM((order, width), f32),
            pltpu.VMEM((2 * width, order), bf16),
            pltpu.VMEM((order, 2 * width), bf16),
            pltpu.VMEM((order, width), f32),
            pltpu.VMEM((order, width), f32),
            pltpu.VMEM((ITERS + 1, rows, width), f32),
            pltpu.VMEM((ITERS, halves, rows, width), f32),
            pltpu.VMEM((ITERS, halves, rows, width), f32),
            pltpu.VMEM((ITERS, 2 * cuts, halves, wide, rows // (2 * cuts), width), f32),
            pltpu.VMEM((ITERS, halves, rows, width), f32),
            pltpu.VMEM((ITERS, halves, rows, width), f32),
            pltpu.VMEM((ITERS, halves, rows, width), f32),
            pltpu.VMEM((ITERS, halves, rows, width), f32),
            pltpu.VMEM((2 * cuts, halves, wide, rows // (2 * cuts), width), f32),
            pltpu.VMEM((ITERS, 2 * cuts, halves, wide, rows // (2 * cuts), width), f32),
            pltpu.VMEM((ITERS, halves, rows, width), f32),
            pltpu.VMEM((ITERS, halves, rows, width), f32),
            pltpu.VMEM((ITERS, 2 * (wbits + nbits) + 1, width, width), f32),
            pltpu.SemaphoreType.DMA((2,)),
            pltpu.SemaphoreType.DMA((copies,)),
            pltpu.SemaphoreType.DMA((copies,)),
        ],
        compiler_params=pltpu.CompilerParams(
            collective_id=0, has_side_effects=True, vmem_limit_bytes=67043328
        ),
    )(places, hamiltonian_tiles, start_vectors)


def solution(mesh):
    return jax.shard_map(
        on_device,
        mesh=mesh,
        in_specs=(P("wide", "narrow"), P("wide", None), P(("wide", "narrow"), None)),
        out_specs=P(("wide", "narrow"), None),
        check_vma=False,
    )
```
